128 devices in a mesh: row: 64 (over z, y, x), pan: 2 (over core).
Axes of the slice: x: 4, y: 4, z: 4, core: 2. Of those that a mesh axis runs over, the one named last changes fastest.
Arguments:
- right_side: float32 [256, 65536], P(None, 'row'), may hold values from -6 to 6
- initial_guess: float32 [256, 65536], P(None, ('row', 'pan')), may hold values from -6 to 6
- v_factor: float32 [128, 128, 16, 512], P('row', None, 'pan'), may hold values from -0.25 to 0.25
- u_factor: float32 [128, 128, 16, 512], P('row', None, 'pan'), may hold values from -0.125 to 0.125
- tile_ranks: int32 [128, 128], P(None, 'row'), may hold values from 0 to 16
- diag_block: float32 [65536, 512], P(('row', 'pan'))
- diag_inverse: float32 [65536, 512], P(('row', 'pan'))
Outputs:
- solution: float32 [256, 65536], P(None, ('row', 'pan'))
- residual: float32 [256, 65536], P(None, ('row', 'pan'))
The draws below stay inside these ranges and needn't reach their ends.
Inputs may be any that keep to these rules, and one draw needn't show every extreme that they name: `tile_ranks`: columns of a tile's factors from its rank on are ignored, as is the low-rank part of tile (i, i).
All inputs are finite; a program needn't handle non-finite values.
Results may differ from the reference program's by a relative error of at most 0.00017.
Values sent between devices are 32-bit elements; how exact they have to be, the bound alone decides.
A program may use at most 64 MiB of HBM per device.

```python
import jax
import jax.numpy as jnp
from jax import lax

B = 512
K = 16
NRHS = 256
ITERS = 2
NT = 128
ORDER = 65536


def draw_diag_block(key, part):
    first_key, second_key = jax.random.split(jax.random.fold_in(key, 11))
    row_pos = jnp.arange(NT * B, dtype=jnp.int32) % B
    col_pos = jnp.arange(B, dtype=jnp.int32)
    identity = (row_pos[:, None] == col_pos[None, :]).astype(jnp.float32)
    spread = jax.random.normal(first_key, (NT * B, B), jnp.float32)
    diagonal = jax.random.uniform(second_key, (NT * B, 1), jnp.float32, 2.0, 4.0)
    return spread * (1.0 / jnp.sqrt(jnp.float32(B))) * (1.0 - identity) + identity * diagonal


def draw_diag_inverse(key, part):
    first_key, second_key = jax.random.split(jax.random.fold_in(key, 23))
    row_pos = jnp.arange(NT * B, dtype=jnp.int32) % B
    col_pos = jnp.arange(B, dtype=jnp.int32)
    identity = (row_pos[:, None] == col_pos[None, :]).astype(jnp.float32)
    spread = jax.random.normal(first_key, (NT * B, B), jnp.float32)
    diagonal = jax.random.uniform(second_key, (NT * B, 1), jnp.float32, 0.2, 0.5)
    return spread * (0.15 / jnp.sqrt(jnp.float32(B))) * (1.0 - identity) + identity * diagonal


def touch_ends(values, own_key, smallest, largest):
    spot = [jax.random.randint(jax.random.fold_in(own_key, axis), (), 0, length) for axis, length in enumerate(values.shape)]
    main_axis = values.shape.index(max(values.shape))
    next_to = spot[:main_axis] + [(spot[main_axis] + 1) % values.shape[main_axis]] + spot[main_axis + 1:]
    return values.at[tuple(spot)].set(smallest).at[tuple(next_to)].set(largest)


def block_scale(rng, dims, cuts, low, high):
    def one(position, shards_of):
        steps = jax.random.uniform(jax.random.fold_in(jax.random.fold_in(rng, 6), position), (shards_of,), jnp.float32, low / len(cuts), high / len(cuts))
        return jnp.repeat(jnp.exp(steps), dims[position] // shards_of).reshape((-1,) + (1,) * (len(dims) - position - 1))

    loudness = one(*cuts[0])
    for cut in cuts[1:]:
        loudness = loudness * one(*cut)
    return loudness


def gaussian(own_key, dims, scale, bound, cuts=(), kind=jnp.bfloat16):
    result = scale * jax.random.normal(own_key, dims, jnp.float32)
    if cuts:
        result = result * block_scale(own_key, dims, cuts, -0.22, 0.18)
    return jnp.clip(result, -bound, bound).astype(kind)


def setup_inputs(seed: int = 0) -> dict:
    streams_of = jax.random.split(jax.random.key(seed), 8)
    return {
        "right_side": gaussian(streams_of[0], (NRHS, ORDER), 1.0, 6.0, ((1, 64),), jnp.float32),
        "initial_guess": gaussian(streams_of[1], (NRHS, ORDER), 1.0, 6.0, ((1, 128),), jnp.float32),
        "v_factor": gaussian(streams_of[2], (NT, NT, K, B), B ** -0.5, 0.25, ((0, 64), (2, 2)), jnp.float32),
        "u_factor": gaussian(streams_of[3], (NT, NT, K, B), (NT * K) ** -0.5, 0.125, ((0, 64), (2, 2)), jnp.float32),
        "tile_ranks": touch_ends(jax.random.randint(streams_of[4], (NT, NT), 0, K + 1), jax.random.fold_in(streams_of[4], 1), 0, K).astype(jnp.int32),
        "diag_block": draw_diag_block(jax.random.fold_in(streams_of[7], 71), 0),
        "diag_inverse": draw_diag_inverse(jax.random.fold_in(streams_of[7], 71), 0),
    }


def reference(right_side, initial_guess, v_factor, u_factor, tile_ranks, diag_block, diag_inverse):
    tile_count = tile_ranks.shape[0]
    tile_width = diag_block.shape[1]
    rank_cap = v_factor.shape[2]
    rhs_count = right_side.shape[0]
    components = jnp.arange(rank_cap, dtype=jnp.int32)
    tile_index = jnp.arange(tile_count, dtype=jnp.int32)
    off_diagonal = tile_index[:, None] != tile_index[None, :]
    rank_mask = ((components[None, None, :] < tile_ranks[:, :, None]) & off_diagonal[:, :, None]).astype(jnp.float32)
    block_rows = diag_block.reshape(tile_count, tile_width, tile_width)
    inverse_rows = diag_inverse.reshape(tile_count, tile_width, tile_width)
    highest = lax.Precision.HIGHEST

    def apply_matrix(guess):
        guess_tiles = guess.reshape(rhs_count, tile_count, tile_width)
        projected = jnp.einsum("jikb,rjb->ijkr", v_factor, guess_tiles, precision=highest)
        projected = projected * rank_mask[:, :, :, None]
        low_rank = jnp.einsum("ijkm,ijkr->rim", u_factor, projected, precision=highest)
        dense_part = jnp.einsum("imb,rib->rim", block_rows, guess_tiles, precision=highest)
        return (low_rank + dense_part).reshape(rhs_count, tile_count * tile_width)

    guess = initial_guess
    residual = right_side
    for iteration in range(ITERS):
        residual = right_side - apply_matrix(guess)
        residual_tiles = residual.reshape(rhs_count, tile_count, tile_width)
        update = jnp.einsum("imb,rib->rim", inverse_rows, residual_tiles, precision=highest)
        guess = guess + update.reshape(rhs_count, tile_count * tile_width)
    return guess, residual
```

```python
import jax
import jax.numpy as jnp
from jax import lax
from jax.experimental import pallas as pl
from jax.experimental.pallas import tpu as pltpu
from jax.sharding import PartitionSpec as P

ITERS = 2
SIDE = 4
GROUPS = 16
BLOCKS = 8
HALF = 8
RANK = 16
WIDTH = 512
RHS = 256
MESH = pl.DeviceIdType.MESH


def halves(x):
    high = x.astype(jnp.bfloat16)
    low = (x - high.astype(jnp.float32)).astype(jnp.bfloat16)
    return high, low


def dot(a, b):
    return jnp.dot(a, b, preferred_element_type=jnp.float32)


def far_first(t):
    return jnp.where(t == 0, 2, jnp.where(t == 1, 1, jnp.where(t == 2, 3, 0)))


def kernel(
    ranks, v_hbm, u_hbm, rhs_hbm, guess_hbm, diag_hbm, inverse_hbm,
    solution_out, residual_out,
    vbuf, ubuf, ut, pbuf, rbuf, diag, inverse, wide, rhs_t, guess_t, gh, gl, dense, acc,
    load_sem, vsend, vrecv, usend, urecv, send_sem, recv_sem,
):
    row = lax.axis_index("row")
    pan = lax.axis_index("pan")
    other = 1 - pan
    tile = row * 2 + pan
    my_x = lax.rem(row, SIDE)
    my_y = lax.rem(row // SIDE, SIDE)
    my_z = row // (SIDE * SIDE)
    my_group = row // SIDE

    loads = [
        pltpu.make_async_copy(v_hbm.at[pan], vbuf.at[:, pan], load_sem.at[0]),
        pltpu.make_async_copy(guess_hbm, wide.at[0], load_sem.at[1]),
        pltpu.make_async_copy(
            rhs_hbm.at[:, pl.ds(pl.multiple_of(pan * WIDTH, WIDTH), WIDTH)], wide.at[1], load_sem.at[2]
        ),
        pltpu.make_async_copy(diag_hbm, diag, load_sem.at[3]),
        pltpu.make_async_copy(inverse_hbm, inverse, load_sem.at[4]),
        pltpu.make_async_copy(u_hbm.at[pan], ubuf.at[:, pan], load_sem.at[5]),
    ]
    for load in loads:
        load.start()

    barrier = pltpu.get_barrier_semaphore()

    def greet(t, carry):
        target = lax.rem(tile + t, GROUPS * BLOCKS)
        pl.semaphore_signal(
            barrier, inc=1, device_id=(target // 2, lax.rem(target, 2)), device_id_type=MESH
        )
        return carry

    lax.fori_loop(1, GROUPS * BLOCKS, greet, 0)

    loads[1].wait()
    start = wide[0].T
    guess_t[...] = start
    high, low = halves(start)
    gh[...] = high
    gl[...] = low

    pl.semaphore_wait(barrier, GROUPS * BLOCKS - 1)

    def group_at(s, sign):
        dz = far_first(s // SIDE)
        dy = far_first(lax.rem(s, SIDE))
        z = lax.rem(my_z + sign * dz + SIDE, SIDE)
        y = lax.rem(my_y + sign * dy + SIDE, SIDE)
        return z * SIDE + y

    def v_piece(g):
        return pltpu.make_async_remote_copy(
            src_ref=v_hbm.at[other, pl.ds(g * BLOCKS, BLOCKS)],
            dst_ref=vbuf.at[pl.ds(g * BLOCKS, BLOCKS), pan],
            send_sem=vsend,
            recv_sem=vrecv.at[g],
            device_id=(row, other),
            device_id_type=MESH,
        )

    def start_piece(s, carry):
        v_piece(group_at(s, 1)).start()
        return carry

    lax.fori_loop(0, GROUPS, start_piece, 0)
    u_swap = pltpu.make_async_remote_copy(
        src_ref=u_hbm.at[other],
        dst_ref=ubuf.at[:, pan],
        send_sem=usend,
        recv_sem=urecv,
        device_id=(row, other),
        device_id_type=MESH,
    )
    u_swap.start()
    loads[0].wait()

    component = lax.broadcasted_iota(jnp.int32, (RANK, RHS), 0)

    for it in range(ITERS):

        def project(s, carry, it=it):
            g = group_at(s, 1)
            if it == 0:
                piece = vbuf.at[pl.ds(g * BLOCKS, BLOCKS), other]
                pltpu.make_async_copy(piece, piece, vrecv.at[g]).wait()
            first = pl.multiple_of(g * BLOCKS, BLOCKS)
            v = vbuf[pl.ds(first, BLOCKS)].reshape(BLOCKS * RANK, WIDTH)
            vh, vl = halves(v)
            p = dot(vh, gh[...]) + dot(vh, gl[...]) + dot(vl, gh[...])
            for b in range(BLOCKS):
                dest = first + b
                rank = jnp.where(dest == tile, 0, ranks[dest, pan])
                pbuf[it, dest] = jnp.where(component < rank, p[b * RANK:(b + 1) * RANK], 0.0)
            for t in range(SIDE):
                shift = (2, 1, 3, 0)[t]
                x = lax.rem(my_x + shift, SIDE)
                to_row = g * SIDE + x
                for core in range(2):
                    to_pan = lax.rem(pan + 1 + core, 2)
                    dest = to_row * 2 + to_pan

                    def remote(to_row=to_row, to_pan=to_pan, dest=dest):
                        pltpu.make_async_remote_copy(
                            src_ref=pbuf.at[it, dest],
                            dst_ref=rbuf.at[it, tile],
                            send_sem=send_sem.at[it],
                            recv_sem=recv_sem.at[it, my_group],
                            device_id=(to_row, to_pan),
                            device_id_type=MESH,
                        ).start()

                    if shift == 0 and core == 1:
                        pl.when(dest != tile)(remote)

                        @pl.when(dest == tile)
                        def _(dest=dest):
                            pltpu.make_async_copy(
                                pbuf.at[it, dest], rbuf.at[it, tile], recv_sem.at[it, my_group]
                            ).start()
                    else:
                        remote()
            return carry

        lax.fori_loop(0, GROUPS, project, 0)

        if it == 0:
            loads[2].wait()
            rhs_t[...] = wide[1].T
            loads[3].wait()
            loads[4].wait()

        def dense_block(b, carry):
            rows = pl.ds(pl.multiple_of(b * 128, 128), 128)
            dh, dl = halves(diag[rows, :])
            dense[rows, :] = rhs_t[rows, :] - (
                dot(dh, gh[...]) + dot(dh, gl[...]) + dot(dl, gh[...])
            )
            return carry

        lax.fori_loop(0, WIDTH // 128, dense_block, 0)

        if it == 0:
            loads[5].wait()
            u_swap.wait_recv()

            def turn(g, carry):
                block = ubuf[pl.ds(pl.multiple_of(g * BLOCKS, BLOCKS), BLOCKS)].reshape(BLOCKS * RANK, WIDTH)
                uh, ul = halves(block.T)
                ut[g, :, 0:128] = uh
                ut[g, :, 128:256] = ul
                return carry

            lax.fori_loop(0, GROUPS, turn, 0)

        acc[...] = jnp.zeros_like(acc)

        def gather(s, carry, it=it):
            g = group_at(s, -1)
            block = rbuf.at[it, pl.ds(g * BLOCKS, BLOCKS)]
            pltpu.make_async_copy(block, block, recv_sem.at[it, g]).wait()
            r = rbuf[it, pl.ds(pl.multiple_of(g * BLOCKS, BLOCKS), BLOCKS)].reshape(BLOCKS * RANK, RHS)
            rh, rl = halves(r)
            both = ut[g]
            acc[...] += dot(both, jnp.concatenate([rh, rh], axis=0)) + dot(both[:, 0:128], rl)
            return carry

        lax.fori_loop(0, GROUPS, gather, 0)

        residual = dense[...] - acc[...]
        acc[...] = residual
        rh, rl = halves(residual)

        def update_block(b, carry):
            rows = pl.ds(pl.multiple_of(b * 128, 128), 128)
            ih, il = halves(inverse[rows, :])
            fresh = guess_t[rows, :] + (dot(ih, gh[...]) + dot(ih, gl[...]) + dot(il, gh[...]))
            guess_t[rows, :] = fresh
            return carry

        gh[...] = rh
        gl[...] = rl
        lax.fori_loop(0, WIDTH // 128, update_block, 0)
        if it < ITERS - 1:
            high, low = halves(guess_t[...])
            gh[...] = high
            gl[...] = low

    residual_out[...] = acc[...].T
    solution_out[...] = guess_t[...].T

    most = pl.ds(0, GROUPS * BLOCKS - 1)
    for it in range(ITERS):
        pltpu.make_async_copy(pbuf.at[it, most], pbuf.at[it, most], send_sem.at[it]).wait()
    pltpu.make_async_copy(v_hbm.at[other], vbuf.at[:, other], vsend).wait()
    u_swap.wait_send()


def on_device(right_side, initial_guess, v_factor, u_factor, tile_ranks, diag_block, diag_inverse):
    f32 = jnp.float32
    bf16 = jnp.bfloat16
    anywhere = pl.BlockSpec(memory_space=pl.ANY)
    vmem = pl.BlockSpec(memory_space=pltpu.VMEM)
    out = jax.ShapeDtypeStruct((RHS, WIDTH), f32)
    tiles = GROUPS * BLOCKS
    return pl.pallas_call(
        kernel,
        out_shape=(out, out),
        in_specs=[pl.BlockSpec(memory_space=pltpu.SMEM)] + [anywhere] * 6,
        out_specs=(vmem, vmem),
        scratch_shapes=[
            pltpu.VMEM((tiles, 2, HALF, WIDTH), f32),
            pltpu.VMEM((tiles, 2, HALF, WIDTH), f32),
            pltpu.VMEM((GROUPS, WIDTH, 256), bf16),
            pltpu.VMEM((ITERS, tiles, RANK, RHS), f32),
            pltpu.VMEM((ITERS, tiles, RANK, RHS), f32),
            pltpu.VMEM((WIDTH, WIDTH), f32),
            pltpu.VMEM((WIDTH, WIDTH), f32),
            pltpu.VMEM((2, RHS, WIDTH), f32),
            pltpu.VMEM((WIDTH, RHS), f32),
            pltpu.VMEM((WIDTH, RHS), f32),
            pltpu.VMEM((WIDTH, RHS), bf16),
            pltpu.VMEM((WIDTH, RHS), bf16),
            pltpu.VMEM((WIDTH, RHS), f32),
            pltpu.VMEM((WIDTH, RHS), f32),
            pltpu.SemaphoreType.DMA((6,)),
            pltpu.SemaphoreType.DMA,
            pltpu.SemaphoreType.DMA((GROUPS,)),
            pltpu.SemaphoreType.DMA,
            pltpu.SemaphoreType.DMA,
            pltpu.SemaphoreType.DMA((ITERS,)),
            pltpu.SemaphoreType.DMA((ITERS, GROUPS)),
        ],
        compiler_params=pltpu.CompilerParams(
            collective_id=0, has_side_effects=True, vmem_limit_bytes=56 * 1024 * 1024
        ),
    )(tile_ranks, v_factor, u_factor, right_side, initial_guess, diag_block, diag_inverse)


def solution(mesh):
    placed = (
        P(None, "row"),
        P(None, ("row", "pan")),
        P("row", None, "pan", None),
        P("row", None, "pan", None),
        P(None, "row"),
        P(("row", "pan"), None),
        P(("row", "pan"), None),
    )
    return jax.shard_map(
        on_device,
        mesh=mesh,
        in_specs=placed,
        out_specs=(P(None, ("row", "pan")), P(None, ("row", "pan"))),
        check_vma=False,
    )
```
